32 devices in a mesh: dp: 2 (over y), seq: 16 (over z, x, core).
Axes of the slice: x: 2, y: 2, z: 4, core: 2. Of those that a mesh axis runs over, the one named last changes fastest.
Arguments:
- tokens: bfloat16 [2, 8192, 1024], P('dp', 'seq'), may hold values from -50 to 50
- w_query: bfloat16 [1024, 1024], P(None, 'dp'), may hold values from -0.1875 to 0.1875
- w_key: bfloat16 [1024, 1024], P(None, 'dp'), may hold values from -0.1875 to 0.1875
- w_value: bfloat16 [1024, 1024], P(None, 'dp'), may hold values from -0.1875 to 0.1875
- w_out: bfloat16 [1024, 1024], P('dp'), may hold values from -0.1875 to 0.1875
- norm_gain: float32 [1024], replicated, may hold values from 0.1 to 1.9
Outputs:
- layer_out: bfloat16 [2, 8192, 1024], P('dp', 'seq')
The draws below stay inside these ranges and needn't reach their ends.
All inputs are finite; a program needn't handle non-finite values.
Results may differ from the reference program's by a relative error of at most 0.017.
Values may be sent and summed in bfloat16 or wider, within the bound.
A program may use at most 128 MiB of HBM per device.

```python
import math
import jax
import jax.numpy as jnp
from jax import lax

D = 1024
H = 8
DH = 128
TOK_DEV = 512
STACKS = 2
SEQ = 8192


def draw_tokens(key, part):
    first, second, third = jax.random.split(jax.random.fold_in(key, 11), 3)
    base = jnp.clip(jax.random.normal(first, (STACKS, SEQ, D), jnp.float32), -4.0, 4.0)
    row_scale = jnp.exp(jax.random.uniform(second, (STACKS, SEQ, 1), jnp.float32, 0.0, math.log(10.0)))
    col_scale = jnp.exp(jax.random.uniform(third, (D,), jnp.float32, 0.0, math.log(10.0)))
    return (base * row_scale * col_scale * 0.1).astype(jnp.bfloat16)


def steps_of(rng, extent, cuts, low, top_value):
    def one(dim, blocks):
        steps = jax.random.uniform(jax.random.fold_in(jax.random.fold_in(rng, 6), dim), (blocks,), jnp.float32, low / len(cuts), top_value / len(cuts))
        return jnp.repeat(jnp.exp(steps), extent[dim] // blocks).reshape((-1,) + (1,) * (len(extent) - dim - 1))

    level = one(*cuts[0])
    for cut in cuts[1:]:
        level = level * one(*cut)
    return level


def scatter_about(own_key, dims, spread, limit, cuts=(), kind=jnp.bfloat16):
    result = spread * jax.random.normal(own_key, dims, jnp.float32)
    if cuts:
        result = result * steps_of(own_key, dims, cuts, -0.22, 0.18)
    return jnp.clip(result, -limit, limit).astype(kind)


def setup_inputs(seed: int = 0) -> dict:
    key_of = jax.random.split(jax.random.key(seed), 7)
    tokens = draw_tokens(jax.random.fold_in(key_of[6], 71), 0)
    w_query = scatter_about(key_of[1], (D, D), D ** -0.5, 0.1875, ((1, 2),))
    w_key = scatter_about(key_of[2], (D, D), D ** -0.5, 0.1875, ((1, 2),))
    w_value = scatter_about(key_of[3], (D, D), D ** -0.5, 0.1875, ((1, 2),))
    w_out = scatter_about(key_of[4], (D, D), D ** -0.5, 0.1875, ((0, 2),))
    norm_gain = jnp.clip(1.0 + 0.18 * jax.random.normal(key_of[5], (D,), jnp.float32), 0.1, 1.9)
    return {"tokens": tokens, "w_query": w_query, "w_key": w_key, "w_value": w_value, "w_out": w_out, "norm_gain": norm_gain}


def rounded(value):
    return lax.optimization_barrier(value.astype(jnp.bfloat16)).astype(jnp.float32)

def inner_block(query_heads, key_heads, value_heads):
    length = query_heads.shape[1]
    block = min(length, 512)
    pieces = []
    for begin in range(0, length, block):
        finish = begin + block
        scores = jnp.einsum('hid,hjd->hij', query_heads[:, begin:finish].astype(jnp.float32), key_heads[:, :finish].astype(jnp.float32))
        row_ids = jnp.arange(begin, finish)[:, None]
        col_ids = jnp.arange(finish)[None, :]
        scores = rounded(jnp.where(col_ids <= row_ids, scores, 0.0))
        pieces.append(jnp.einsum('hij,hje->hie', scores, value_heads[:, :finish].astype(jnp.float32)))
    return jnp.concatenate(pieces, axis=1)

def reference(tokens, w_query, w_key, w_value, w_out, norm_gain):
    gain_heads = norm_gain.reshape(H, 1, DH)

    def one_stack(rows):

        def heads(weight):
            proj = jnp.dot(rows, weight, preferred_element_type=jnp.float32).astype(jnp.bfloat16)
            return proj.reshape(SEQ // TOK_DEV, TOK_DEV, H, DH).transpose(0, 2, 1, 3)
        blocks = (heads(w_query), heads(w_key), heads(w_value))

        def step(state, block):
            query_heads, key_heads, value_heads = block
            carried = jnp.einsum('htd,hde->hte', query_heads.astype(jnp.float32), rounded(state))
            mixed_raw = inner_block(query_heads, key_heads, value_heads) + carried
            scale = lax.rsqrt(lax.optimization_barrier(jnp.mean(mixed_raw * mixed_raw, axis=-1, keepdims=True)) + 1e-05)
            normed = (mixed_raw * scale * gain_heads).astype(jnp.bfloat16)
            state = state + jnp.einsum('htd,hte->hde', key_heads.astype(jnp.float32), value_heads.astype(jnp.float32))
            return (state, normed)
        start_state = jnp.zeros((H, DH, DH), jnp.float32)
        _, normed = lax.scan(step, start_state, blocks)
        normed = normed.transpose(0, 2, 1, 3).reshape(SEQ, D)
        return jnp.dot(normed, w_out, preferred_element_type=jnp.float32).astype(jnp.bfloat16)
    return lax.map(one_stack, tokens)
```

```python
import functools

import jax
import jax.numpy as jnp
from jax import lax
from jax.experimental import pallas as pl
from jax.experimental.pallas import tpu as pltpu
from jax.sharding import PartitionSpec as P

H = 8
DH = 128
GROUP = 4
MESH = pl.DeviceIdType.MESH
F32 = jnp.float32
BF16 = jnp.bfloat16


class Scan:
    def __init__(self, seq, steps, state, total, before, send, recv, prior, fin, send_sem, recv_sem):
        self.seq, self.steps = seq, steps
        self.state, self.total, self.before = state, total, before
        self.send, self.recv, self.prior, self.fin = send, recv, prior, fin
        self.send_sem, self.recv_sem = send_sem, recv_sem
        self.half = state.shape[0] // 2
        self.core = lax.rem(seq, 2)
        self.mine = pl.ds(pl.multiple_of(self.core * self.half, 16), self.half)
        self.other = pl.ds(pl.multiple_of((1 - self.core) * self.half, 16), self.half)
        self.at = 0
        self.copies = []

    def bit(self, step):
        return lax.rem(self.seq // (1 << step), 2)

    def partner(self, step):
        return self.seq + (1 - 2 * self.bit(step)) * (1 << step)

    def push(self, src, dst, index, step):
        copy = pltpu.make_async_remote_copy(
            src_ref=src,
            dst_ref=dst,
            send_sem=self.send_sem.at[index],
            recv_sem=self.recv_sem.at[index],
            device_id={"seq": self.partner(step)},
            device_id_type=MESH,
        )
        copy.start()
        self.copies.append(copy)

    def begin(self):
        self.send[0] = self.state[self.other, :].astype(BF16)
        self.push(self.send.at[0], self.recv.at[0], 0, 0)

    def advance(self):
        step = self.at
        if step > self.steps:
            return
        self.at += 1
        self.copies[step].wait_recv()
        if step == self.steps:
            return
        came = self.recv[step].astype(F32)
        if step == 0:
            self.total[...] = self.state[self.mine, :] + came
            self.before[...] = jnp.zeros(self.before.shape, F32)
        else:
            self.before[...] += jnp.where(self.bit(step) == 1, came, 0.0)
            if step < self.steps - 1:
                self.total[...] += came
        if step < self.steps - 1:
            self.send[step + 1] = self.total[...].astype(BF16)
            self.push(self.send.at[step + 1], self.recv.at[step + 1], step + 1, step + 1)
        else:
            before = self.before[...]
            first = self.recv[0].astype(F32)
            extra = jnp.where(self.core == 0, self.state[self.mine, :], 0.0)
            self.fin[...] = (before + extra).astype(BF16)
            self.push(self.fin, self.prior.at[self.mine, :], self.steps, 0)
            self.prior[self.mine, :] = (before + jnp.where(self.core == 1, first, 0.0)).astype(BF16)

    def drain(self):
        while self.at <= self.steps:
            self.advance()

    def close(self):
        for copy in self.copies:
            copy.wait_send()


def kernel(
    n, steps, sub,
    tok_hbm, wq_hbm, wk_hbm, wv_hbm, wo_hbm, gain_ref, out_ref,
    tok, own, own_o, wide, wide_o, kvq, within, normed, acc,
    state_a, total_a, before_a, send_a, recv_a, prior_a, fin_a,
    state_b, total_b, before_b, send_b, recv_b, prior_b, fin_b,
    load_sem, y_send, y_recv, x_send, x_recv, c_send, c_recv, d_send, d_recv,
    as_send, as_recv, bs_send, bs_recv,
):
    dp, seq = lax.axis_index("dp"), lax.axis_index("seq")
    length, width = tok.shape
    cols = own.shape[2]
    heads = cols // DH
    sources = [wk_hbm, wv_hbm, wq_hbm, wo_hbm]
    rank = lax.rem(seq, GROUP)
    core = lax.rem(seq, 2)
    xbit = lax.rem(seq // 2, 2)
    core_mate = seq + 1 - 2 * core
    x_mate = seq + 2 * (1 - 2 * xbit)
    x_rank = rank + 2 * (1 - 2 * xbit)

    loads = [pltpu.make_async_copy(tok_hbm, tok, load_sem.at[4])]
    for kind in range(4):
        dst = own.at[kind] if kind < 3 else own_o
        loads.append(pltpu.make_async_copy(sources[kind], dst, load_sem.at[kind]))
    for copy in loads:
        copy.start()

    barrier = pltpu.get_barrier_semaphore()
    for slot in range(1, n):
        pl.semaphore_signal(barrier, inc=1, device_id={"dp": lax.rem(dp + slot, n)}, device_id_type=MESH)
    for step in range(steps):
        bit = lax.rem(seq // (1 << step), 2)
        mate = seq + (1 - 2 * bit) * (1 << step)
        pl.semaphore_signal(barrier, inc=1, device_id={"seq": mate}, device_id_type=MESH)
    pl.semaphore_wait(barrier, n - 1 + steps)

    def rows_of(kind, who, s):
        quarter = sources[kind].shape[0] // GROUP
        size = quarter // sub
        return pl.ds(pl.multiple_of(who * quarter + s * size, 16), size)

    def place(kind, slot, rows):
        if kind < 3:
            return wide.at[slot - 1, kind, rows, :]
        return wide_o.at[slot - 1, rows, :]

    pieces = [[(kind, slot, s) for s in range(sub) for slot in range(1, n)] for kind in range(4)]
    remote, sent = {}, []

    def push(src, dst, send, recv, target):
        copy = pltpu.make_async_remote_copy(
            src_ref=src, dst_ref=dst, send_sem=send, recv_sem=recv, device_id=target, device_id_type=MESH
        )
        copy.start()
        sent.append(copy)
        return copy

    for kind in range(4):
        for piece in pieces[kind]:
            _, slot, s = piece
            index = (kind, slot - 1, s)
            rows = rows_of(kind, rank, s)
            remote["y", piece] = push(
                sources[kind].at[rows, :], place(kind, slot, rows), y_send.at[index], y_recv.at[index],
                {"dp": lax.rem(dp - slot + n, n)},
            )

    def relay(piece):
        kind, slot, s = piece
        index = (kind, slot - 1, s)
        here = place(kind, slot, rows_of(kind, rank, s))
        remote["y", piece].wait_recv()
        remote["x", piece] = push(here, here, x_send.at[index], x_recv.at[index], {"seq": x_mate})
        remote["c", piece] = push(here, here, c_send.at[index], c_recv.at[index], {"seq": core_mate})

    def relay_again(piece):
        kind, slot, s = piece
        index = (kind, slot - 1, s)
        here = place(kind, slot, rows_of(kind, x_rank, s))
        remote["x", piece].wait_recv()
        remote["d", piece] = push(here, here, d_send.at[index], d_recv.at[index], {"seq": core_mate})

    order = [piece for kind in range(4) for piece in pieces[kind]]
    half_of = len(pieces[0]) // 2 or 1
    cuts = []
    for kind in range(4):
        base = kind * len(pieces[0])
        cuts.append(base + half_of)
        cuts.append(base + len(pieces[0]))
    done = {"first": 0, "again": 0}

    def pump(first, again):
        first = cuts[first - 1] if first else 0
        again = cuts[again - 1] if again else 0
        while done["first"] < first or done["again"] < again:
            if done["again"] < again and done["again"] < done["first"] - 1 or done["first"] >= first:
                relay_again(order[done["again"]])
                done["again"] += 1
            else:
                relay(order[done["first"]])
                done["first"] += 1

    def ready(kind):
        for piece in pieces[kind]:
            remote["c", piece].wait_recv()
            remote["d", piece].wait_recv()

    chunk = min(256, cols)

    def project(kind, slot):
        source = own.at[kind] if slot == 0 else wide.at[slot - 1, kind]

        @pl.loop(0, cols // chunk)
        def _(i):
            at = pl.ds(pl.multiple_of(i * chunk, 128), chunk)
            kvq[kind, slot, :, at] = jnp.dot(tok[...], source[:, at], preferred_element_type=F32).astype(BF16)

    def states(slot, ref, base):
        @pl.loop(0, heads)
        def _(h):
            at = pl.ds(pl.multiple_of(h * DH, DH), DH)
            ref[pl.ds(pl.multiple_of(base + h * DH, DH), DH), :] = lax.dot_general(
                kvq[0, slot, :, at], kvq[1, slot, :, at], (((0,), (0,)), ((), ())), preferred_element_type=F32
            )

    half = length // 2

    def inner(slot):
        @pl.loop(0, heads)
        def _(h):
            at = pl.ds(pl.multiple_of(h * DH, DH), DH)
            for begin in (0, half):
                end = begin + half
                scores = lax.dot_general(
                    kvq[2, slot, begin:end, at], kvq[0, slot, :end, at], (((1,), (1,)), ((), ())),
                    preferred_element_type=F32,
                )
                row = begin + lax.broadcasted_iota(jnp.int32, (half, end), 0)
                col = lax.broadcasted_iota(jnp.int32, (half, end), 1)
                scores = jnp.where(col <= row, scores, 0.0).astype(BF16)
                within[slot, begin:end, at] = jnp.dot(
                    scores, kvq[1, slot, :end, at], preferred_element_type=F32
                )

    def finish(slot, prior, base):
        owner = lax.rem(dp + slot, n)

        @pl.loop(0, heads)
        def _(h):
            at = pl.ds(pl.multiple_of(h * DH, DH), DH)
            carried = jnp.dot(
                kvq[2, slot, :, at], prior[pl.ds(pl.multiple_of(base + h * DH, DH), DH), :],
                preferred_element_type=F32,
            )
            mixed = within[slot, :, at] + carried
            scale = lax.rsqrt(jnp.sum(mixed * mixed, axis=-1, keepdims=True) * (1.0 / DH) + 1e-05)
            normed[slot, :, at] = (mixed * scale * gain_ref[pl.ds(owner * heads + h, 1), :]).astype(BF16)

    def join(slot):
        source = own_o if slot == 0 else wide_o.at[slot - 1]

        @pl.loop(0, width // 256)
        def _(i):
            at = pl.ds(pl.multiple_of(i * 256, 128), 256)
            part = jnp.dot(normed[slot], source[:, at], preferred_element_type=F32)
            if slot > 0:
                part = acc[:, at] + part
            if slot == n - 1:
                out_ref[:, at] = part.astype(BF16)
            else:
                acc[:, at] = part

    scan_a = Scan(seq, steps, state_a, total_a, before_a, send_a, recv_a, prior_a, fin_a, as_send, as_recv)
    scan_b = Scan(seq, steps, state_b, total_b, before_b, send_b, recv_b, prior_b, fin_b, bs_send, bs_recv)

    loads[0].wait()
    loads[1].wait()
    project(0, 0)
    loads[2].wait()
    project(1, 0)
    states(0, state_a, 0)
    scan_a.begin()
    pump(1, 0)
    loads[3].wait()
    project(2, 0)
    pump(2, 1)
    scan_a.advance()
    inner(0)
    pump(3, 2)
    scan_a.advance()
    ready(0)
    for slot in range(1, n):
        project(0, slot)
    pump(4, 3)
    scan_a.advance()
    pump(4, 4)
    ready(1)
    for slot in range(1, n):
        project(1, slot)
        states(slot, state_b, (slot - 1) * cols)
    scan_b.begin()
    scan_a.advance()
    pump(5, 4)
    scan_b.advance()
    scan_a.drain()
    finish(0, prior_a, 0)
    pump(6, 5)
    scan_b.advance()
    loads[4].wait()
    join(0)
    pump(7, 6)
    scan_b.advance()
    ready(2)
    for slot in range(1, n):
        project(2, slot)
        inner(slot)
    pump(8, 7)
    scan_b.advance()
    scan_b.drain()
    for slot in range(1, n):
        finish(slot, prior_b, (slot - 1) * cols)
    pump(8, 8)
    ready(3)
    for slot in range(1, n):
        join(slot)
    for copy in sent:
        copy.wait_send()
    scan_a.close()
    scan_b.close()


def body(n, seqs, tokens, w_query, w_key, w_value, w_out, norm_gain):
    length, width = tokens.shape[1:]
    cols = w_query.shape[1]
    depth = w_out.shape[0]
    steps = seqs.bit_length() - 1
    sub = 2 if n <= 2 else 1
    any_spec = pl.BlockSpec(memory_space=pl.ANY)
    vmem = pl.BlockSpec(memory_space=pltpu.VMEM)
    scans = []
    for rows in (cols, (n - 1) * cols):
        part = rows // 2
        scans += [
            pltpu.VMEM((rows, DH), F32),
            pltpu.VMEM((part, DH), F32),
            pltpu.VMEM((part, DH), F32),
            pltpu.VMEM((steps, part, DH), BF16),
            pltpu.VMEM((steps, part, DH), BF16),
            pltpu.VMEM((rows, DH), BF16),
            pltpu.VMEM((part, DH), BF16),
        ]
    out = pl.pallas_call(
        functools.partial(kernel, n, steps, sub),
        out_shape=jax.ShapeDtypeStruct((length, width), BF16),
        in_specs=[any_spec] * 5 + [vmem],
        out_specs=vmem,
        scratch_shapes=[
            pltpu.VMEM((length, width), BF16),
            pltpu.VMEM((3, width, cols), BF16),
            pltpu.VMEM((depth, width), BF16),
            pltpu.VMEM((n - 1, 3, width, cols), BF16),
            pltpu.VMEM((n - 1, depth, width), BF16),
            pltpu.VMEM((3, n, length, cols), BF16),
            pltpu.VMEM((n, length, cols), F32),
            pltpu.VMEM((n, length, cols), BF16),
            pltpu.VMEM((length, width), F32),
        ]
        + scans
        + [pltpu.SemaphoreType.DMA((5,))]
        + [pltpu.SemaphoreType.DMA((4, n - 1, sub))] * 8
        + [pltpu.SemaphoreType.DMA((steps + 1,))] * 4,
        compiler_params=pltpu.CompilerParams(
            collective_id=0, has_side_effects=True, vmem_limit_bytes=50 * 1024 * 1024
        ),
    )(tokens[0], w_query, w_key, w_value, w_out, norm_gain.reshape(-1, DH))
    return out[None]


def solution(mesh):
    in_specs = (
        P("dp", "seq", None),
        P(None, "dp"),
        P(None, "dp"),
        P(None, "dp"),
        P("dp", None),
        P(),
    )
    out_specs = P("dp", "seq", None)
    fn = functools.partial(body, mesh.shape["dp"], mesh.shape["seq"])
    return jax.shard_map(fn, mesh=mesh, in_specs=in_specs, out_specs=out_specs, check_vma=False)
```

```python
import functools

import jax
import jax.numpy as jnp
from jax import lax
from jax.experimental import pallas as pl
from jax.experimental.pallas import tpu as pltpu
from jax.sharding import PartitionSpec as P

H = 8
DH = 128
GROUP = 8
MESH = pl.DeviceIdType.MESH
F32 = jnp.float32
BF16 = jnp.bfloat16


class Scan:
    def __init__(self, seq, steps, state, total, before, send, recv, prior, fin, send_sem, recv_sem):
        self.seq, self.steps = seq, steps
        self.state, self.total, self.before = state, total, before
        self.send, self.recv, self.prior, self.fin = send, recv, prior, fin
        self.send_sem, self.recv_sem = send_sem, recv_sem
        self.half = state.shape[0] // 2
        self.core = lax.rem(seq, 2)
        self.mine = pl.ds(pl.multiple_of(self.core * self.half, 16), self.half)
        self.other = pl.ds(pl.multiple_of((1 - self.core) * self.half, 16), self.half)
        self.at = 0
        self.copies = []

    def bit(self, step):
        return lax.rem(self.seq // (1 << step), 2)

    def partner(self, step):
        return self.seq + (1 - 2 * self.bit(step)) * (1 << step)

    def push(self, src, dst, index, step):
        copy = pltpu.make_async_remote_copy(
            src_ref=src,
            dst_ref=dst,
            send_sem=self.send_sem.at[index],
            recv_sem=self.recv_sem.at[index],
            device_id={"seq": self.partner(step)},
            device_id_type=MESH,
        )
        copy.start()
        self.copies.append(copy)

    def begin(self):
        self.send[0] = self.state[self.other, :].astype(BF16)
        self.push(self.send.at[0], self.recv.at[0], 0, 0)

    def advance(self):
        step = self.at
        if step > self.steps:
            return
        self.at += 1
        self.copies[step].wait_recv()
        if step == self.steps:
            return
        came = self.recv[step].astype(F32)
        if step == 0:
            self.total[...] = self.state[self.mine, :] + came
            self.before[...] = jnp.zeros(self.before.shape, F32)
        else:
            self.before[...] += jnp.where(self.bit(step) == 1, came, 0.0)
            if step < self.steps - 1:
                self.total[...] += came
        if step < self.steps - 1:
            self.send[step + 1] = self.total[...].astype(BF16)
            self.push(self.send.at[step + 1], self.recv.at[step + 1], step + 1, step + 1)
        else:
            before = self.before[...]
            first = self.recv[0].astype(F32)
            extra = jnp.where(self.core == 0, self.state[self.mine, :], 0.0)
            self.fin[...] = (before + extra).astype(BF16)
            self.push(self.fin, self.prior.at[self.mine, :], self.steps, 0)
            self.prior[self.mine, :] = (before + jnp.where(self.core == 1, first, 0.0)).astype(BF16)

    def drain(self):
        while self.at <= self.steps:
            self.advance()

    def close(self):
        for copy in self.copies:
            copy.wait_send()


def kernel(
    n, steps, sub,
    tok_hbm, wq_hbm, wk_hbm, wv_hbm, wo_hbm, gain_ref, out_ref,
    tok, own, own_o, wide, wide_o, kvq, within, normed, acc,
    state_a, total_a, before_a, send_a, recv_a, prior_a, fin_a,
    state_b, total_b, before_b, send_b, recv_b, prior_b, fin_b,
    load_sem, sends, recvs,
    as_send, as_recv, bs_send, bs_recv,
):
    dp, seq = lax.axis_index("dp"), lax.axis_index("seq")
    length, width = tok.shape
    cols = own.shape[2]
    heads = cols // DH
    sources = [wk_hbm, wv_hbm, wq_hbm, wo_hbm]
    rank = lax.rem(seq, GROUP)
    core = lax.rem(seq, 2)
    xbit = lax.rem(seq // 2, 2)
    core_mate = seq + 1 - 2 * core
    x_mate = seq + 2 * (1 - 2 * xbit)
    zbit = lax.rem(seq // 4, 2)
    z_mate = seq + 4 * (1 - 2 * zbit)
    x_rank = rank + 2 * (1 - 2 * xbit)
    z_rank = rank + 4 * (1 - 2 * zbit)
    g_rank = z_rank + 2 * (1 - 2 * xbit)
    lanes = ("y", "x", "z", "g", "c0", "c1", "c2", "c3")

    loads = [pltpu.make_async_copy(tok_hbm, tok, load_sem.at[4])]
    for kind in range(4):
        dst = own.at[kind] if kind < 3 else own_o
        loads.append(pltpu.make_async_copy(sources[kind], dst, load_sem.at[kind]))
    for copy in loads:
        copy.start()

    barrier = pltpu.get_barrier_semaphore()
    for slot in range(1, n):
        pl.semaphore_signal(barrier, inc=1, device_id={"dp": lax.rem(dp + slot, n)}, device_id_type=MESH)
    for step in range(steps):
        bit = lax.rem(seq // (1 << step), 2)
        mate = seq + (1 - 2 * bit) * (1 << step)
        pl.semaphore_signal(barrier, inc=1, device_id={"seq": mate}, device_id_type=MESH)
    pl.semaphore_wait(barrier, n - 1 + steps)

    def rows_of(kind, who, s):
        quarter = sources[kind].shape[0] // GROUP
        size = quarter // sub
        return pl.ds(pl.multiple_of(who * quarter + s * size, 16), size)

    def place(kind, slot, rows):
        if kind < 3:
            return wide.at[slot - 1, kind, rows, :]
        return wide_o.at[slot - 1, rows, :]

    pieces = [[(kind, slot, s) for s in range(sub) for slot in range(1, n)] for kind in range(4)]
    remote, sent = {}, []

    def push(src, dst, send, recv, target):
        copy = pltpu.make_async_remote_copy(
            src_ref=src, dst_ref=dst, send_sem=send, recv_sem=recv, device_id=target, device_id_type=MESH
        )
        copy.start()
        sent.append(copy)
        return copy

    for kind in range(4):
        for piece in pieces[kind]:
            _, slot, s = piece
            index = (0, kind, slot - 1, s)
            rows = rows_of(kind, rank, s)
            remote["y", piece] = push(
                sources[kind].at[rows, :], place(kind, slot, rows), sends.at[index], recvs.at[index],
                {"dp": lax.rem(dp - slot + n, n)},
            )

    def forward(name, piece, who, target):
        kind, slot, s = piece
        here = place(kind, slot, rows_of(kind, who, s))
        index = (lanes.index(name), kind, slot - 1, s)
        remote[name, piece] = push(here, here, sends.at[index], recvs.at[index], target)

    def relay(piece):
        remote["y", piece].wait_recv()
        forward("x", piece, rank, {"seq": x_mate})
        forward("z", piece, rank, {"seq": z_mate})
        forward("c0", piece, rank, {"seq": core_mate})

    def relay_again(piece):
        even = (piece[1] + piece[2]) % 2 == 1
        remote["x", piece].wait_recv()
        if even:
            forward("g", piece, x_rank, {"seq": z_mate})
        forward("c1", piece, x_rank, {"seq": core_mate})
        remote["z", piece].wait_recv()
        if not even:
            forward("g", piece, z_rank, {"seq": x_mate})
        forward("c2", piece, z_rank, {"seq": core_mate})

    def relay_last(piece):
        remote["g", piece].wait_recv()
        forward("c3", piece, g_rank, {"seq": core_mate})

    order = [piece for kind in range(4) for piece in pieces[kind]]
    half_of = len(pieces[0]) // 2 or 1
    cuts = [0]
    for kind in range(4):
        base = kind * len(pieces[0])
        cuts += [base + half_of, base + len(pieces[0])]
    acts = (relay, relay_again, relay_last)
    done = [0, 0, 0]

    def pump(*goals):
        goals = [cuts[goal] for goal in goals]
        while any(at < goal for at, goal in zip(done, goals)):
            todo = [i for i in range(3) if done[i] < goals[i] and (i == 0 or done[i] < done[i - 1])]
            pick = min(todo, key=lambda i: (done[i] + i, -i))
            acts[pick](order[done[pick]])
            done[pick] += 1

    def ready(kind):
        for piece in pieces[kind]:
            for name in ("c0", "c1", "c2", "c3"):
                remote[name, piece].wait_recv()

    chunk = min(256, cols)

    def project(kind, slot):
        source = own.at[kind] if slot == 0 else wide.at[slot - 1, kind]

        @pl.loop(0, cols // chunk)
        def _(i):
            at = pl.ds(pl.multiple_of(i * chunk, 128), chunk)
            kvq[kind, slot, :, at] = jnp.dot(tok[...], source[:, at], preferred_element_type=F32).astype(BF16)

    def states(slot, ref, base):
        @pl.loop(0, heads)
        def _(h):
            at = pl.ds(pl.multiple_of(h * DH, DH), DH)
            ref[pl.ds(pl.multiple_of(base + h * DH, DH), DH), :] = lax.dot_general(
                kvq[0, slot, :, at], kvq[1, slot, :, at], (((0,), (0,)), ((), ())), preferred_element_type=F32
            )

    half = length // 2

    def inner(slot):
        @pl.loop(0, heads)
        def _(h):
            at = pl.ds(pl.multiple_of(h * DH, DH), DH)
            for begin in (0, half):
                end = begin + half
                scores = lax.dot_general(
                    kvq[2, slot, begin:end, at], kvq[0, slot, :end, at], (((1,), (1,)), ((), ())),
                    preferred_element_type=F32,
                )
                row = begin + lax.broadcasted_iota(jnp.int32, (half, end), 0)
                col = lax.broadcasted_iota(jnp.int32, (half, end), 1)
                scores = jnp.where(col <= row, scores, 0.0).astype(BF16)
                within[slot, begin:end, at] = jnp.dot(
                    scores, kvq[1, slot, :end, at], preferred_element_type=F32
                )

    def finish(slot, prior, base):
        owner = lax.rem(dp + slot, n)

        @pl.loop(0, heads)
        def _(h):
            at = pl.ds(pl.multiple_of(h * DH, DH), DH)
            carried = jnp.dot(
                kvq[2, slot, :, at], prior[pl.ds(pl.multiple_of(base + h * DH, DH), DH), :],
                preferred_element_type=F32,
            )
            mixed = within[slot, :, at] + carried
            scale = lax.rsqrt(jnp.sum(mixed * mixed, axis=-1, keepdims=True) * (1.0 / DH) + 1e-05)
            normed[slot, :, at] = (mixed * scale * gain_ref[pl.ds(owner * heads + h, 1), :]).astype(BF16)

    def join(slot):
        source = own_o if slot == 0 else wide_o.at[slot - 1]

        @pl.loop(0, width // 256)
        def _(i):
            at = pl.ds(pl.multiple_of(i * 256, 128), 256)
            part = jnp.dot(normed[slot], source[:, at], preferred_element_type=F32)
            if slot > 0:
                part = acc[:, at] + part
            if slot == n - 1:
                out_ref[:, at] = part.astype(BF16)
            else:
                acc[:, at] = part

    scan_a = Scan(seq, steps, state_a, total_a, before_a, send_a, recv_a, prior_a, fin_a, as_send, as_recv)
    scan_b = Scan(seq, steps, state_b, total_b, before_b, send_b, recv_b, prior_b, fin_b, bs_send, bs_recv)

    others = range(1, n)
    loads[0].wait()
    loads[1].wait()
    project(0, 0)
    pump(1, 0, 0)
    loads[2].wait()
    project(1, 0)
    states(0, state_a, 0)
    scan_a.begin()
    pump(2, 1, 0)
    loads[3].wait()
    project(2, 0)
    pump(3, 2, 1)
    scan_a.advance()
    inner(0)
    pump(4, 3, 2)
    scan_a.advance()
    ready(0)
    for slot in others:
        project(0, slot)
    pump(5, 4, 3)
    scan_a.advance()
    pump(5, 5, 4)
    ready(1)
    for slot in others:
        project(1, slot)
        states(slot, state_b, (slot - 1) * cols)
    scan_b.begin()
    scan_a.advance()
    pump(6, 5, 5)
    scan_b.advance()
    scan_a.drain()
    finish(0, prior_a, 0)
    pump(7, 6, 5)
    scan_b.advance()
    loads[4].wait()
    join(0)
    pump(8, 7, 6)
    scan_b.advance()
    ready(2)
    for slot in others:
        project(2, slot)
    pump(8, 8, 7)
    scan_b.advance()
    for slot in others:
        inner(slot)
    pump(8, 8, 8)
    scan_b.drain()
    for slot in others:
        finish(slot, prior_b, (slot - 1) * cols)
    ready(3)
    for slot in others:
        join(slot)
    for copy in sent:
        copy.wait_send()
    scan_a.close()
    scan_b.close()


def body(n, seqs, tokens, w_query, w_key, w_value, w_out, norm_gain):
    length, width = tokens.shape[1:]
    cols = w_query.shape[1]
    depth = w_out.shape[0]
    steps = seqs.bit_length() - 1
    sub = 2 if n <= 2 else 1
    any_spec = pl.BlockSpec(memory_space=pl.ANY)
    vmem = pl.BlockSpec(memory_space=pltpu.VMEM)
    scans = []
    for rows in (cols, (n - 1) * cols):
        part = rows // 2
        scans += [
            pltpu.VMEM((rows, DH), F32),
            pltpu.VMEM((part, DH), F32),
            pltpu.VMEM((part, DH), F32),
            pltpu.VMEM((steps, part, DH), BF16),
            pltpu.VMEM((steps, part, DH), BF16),
            pltpu.VMEM((rows, DH), BF16),
            pltpu.VMEM((part, DH), BF16),
        ]
    out = pl.pallas_call(
        functools.partial(kernel, n, steps, sub),
        out_shape=jax.ShapeDtypeStruct((length, width), BF16),
        in_specs=[any_spec] * 5 + [vmem],
        out_specs=vmem,
        scratch_shapes=[
            pltpu.VMEM((length, width), BF16),
            pltpu.VMEM((3, width, cols), BF16),
            pltpu.VMEM((depth, width), BF16),
            pltpu.VMEM((n - 1, 3, width, cols), BF16),
            pltpu.VMEM((n - 1, depth, width), BF16),
            pltpu.VMEM((3, n, length, cols), BF16),
            pltpu.VMEM((n, length, cols), F32),
            pltpu.VMEM((n, length, cols), BF16),
            pltpu.VMEM((length, width), F32),
        ]
        + scans
        + [pltpu.SemaphoreType.DMA((5,))]
        + [pltpu.SemaphoreType.DMA((8, 4, n - 1, sub))] * 2
        + [pltpu.SemaphoreType.DMA((steps + 1,))] * 4,
        compiler_params=pltpu.CompilerParams(
            collective_id=0, has_side_effects=True, vmem_limit_bytes=67043328
        ),
    )(tokens[0], w_query, w_key, w_value, w_out, norm_gain.reshape(-1, DH))
    return out[None]


def solution(mesh):
    in_specs = (
        P("dp", "seq", None),
        P(None, "dp"),
        P(None, "dp"),
        P(None, "dp"),
        P("dp", None),
        P(),
    )
    out_specs = P("dp", "seq", None)
    fn = functools.partial(body, mesh.shape["dp"], mesh.shape["seq"])
    return jax.shard_map(fn, mesh=mesh, in_specs=in_specs, out_specs=out_specs, check_vma=False)
```

```python
import functools

import jax
import jax.numpy as jnp
from jax import lax
from jax.experimental import pallas as pl
from jax.experimental.pallas import tpu as pltpu
from jax.sharding import PartitionSpec as P

H = 8
DH = 128
GROUP = 8
MESH = pl.DeviceIdType.MESH
F32 = jnp.float32
BF16 = jnp.bfloat16


class Scan:
    def __init__(self, seq, steps, state, total, before, send, recv, prior, fin, send_sem, recv_sem):
        self.seq, self.steps = seq, steps
        self.state, self.total, self.before = state, total, before
        self.send, self.recv, self.prior, self.fin = send, recv, prior, fin
        self.send_sem, self.recv_sem = send_sem, recv_sem
        self.half = state.shape[0] // 2
        self.core = lax.rem(seq, 2)
        self.mine = pl.ds(pl.multiple_of(self.core * self.half, 16), self.half)
        self.other = pl.ds(pl.multiple_of((1 - self.core) * self.half, 16), self.half)
        self.at = 0
        self.copies = []

    def bit(self, step):
        return lax.rem(self.seq // (1 << step), 2)

    def partner(self, step):
        return self.seq + (1 - 2 * self.bit(step)) * (1 << step)

    def push(self, src, dst, index, step):
        copy = pltpu.make_async_remote_copy(
            src_ref=src,
            dst_ref=dst,
            send_sem=self.send_sem.at[index],
            recv_sem=self.recv_sem.at[index],
            device_id={"seq": self.partner(step)},
            device_id_type=MESH,
        )
        copy.start()
        self.copies.append(copy)

    def begin(self):
        self.send[0] = self.state[self.other, :].astype(BF16)
        self.push(self.send.at[0], self.recv.at[0], 0, 0)

    def advance(self):
        step = self.at
        if step > self.steps:
            return
        self.at += 1
        self.copies[step].wait_recv()
        if step == self.steps:
            return
        came = self.recv[step].astype(F32)
        if step == 0:
            self.total[...] = self.state[self.mine, :] + came
            self.before[...] = jnp.zeros(self.before.shape, F32)
        else:
            self.before[...] += jnp.where(self.bit(step) == 1, came, 0.0)
            if step < self.steps - 1:
                self.total[...] += came
        if step < self.steps - 1:
            self.send[step + 1] = self.total[...].astype(BF16)
            self.push(self.send.at[step + 1], self.recv.at[step + 1], step + 1, step + 1)
        else:
            before = self.before[...]
            first = self.recv[0].astype(F32)
            extra = jnp.where(self.core == 0, self.state[self.mine, :], 0.0)
            self.fin[...] = (before + extra).astype(BF16)
            self.push(self.fin, self.prior.at[self.mine, :], self.steps, 0)
            self.prior[self.mine, :] = (before + jnp.where(self.core == 1, first, 0.0)).astype(BF16)

    def drain(self):
        while self.at <= self.steps:
            self.advance()

    def close(self):
        for copy in self.copies:
            copy.wait_send()


def kernel(
    n, steps, sub,
    tok_hbm, wq_hbm, wk_hbm, wv_hbm, wo_hbm, gain_ref, out_ref,
    tok, own, own_o, wide, wide_o, kvq, within, normed, acc,
    state_a, total_a, before_a, send_a, recv_a, prior_a, fin_a,
    state_b, total_b, before_b, send_b, recv_b, prior_b, fin_b,
    load_sem, sends, recvs,
    as_send, as_recv, bs_send, bs_recv,
):
    dp, seq = lax.axis_index("dp"), lax.axis_index("seq")
    length, width = tok.shape
    cols = own.shape[2]
    heads = cols // DH
    sources = [wk_hbm, wv_hbm, wq_hbm, wo_hbm]
    rank = lax.rem(seq, GROUP)
    core = lax.rem(seq, 2)
    xbit = lax.rem(seq // 2, 2)
    core_mate = seq + 1 - 2 * core
    x_mate = seq + 2 * (1 - 2 * xbit)
    zbit = lax.rem(seq // 4, 2)
    z_mate = seq + 4 * (1 - 2 * zbit)
    x_rank = rank + 2 * (1 - 2 * xbit)
    z_rank = rank + 4 * (1 - 2 * zbit)
    g_rank = z_rank + 2 * (1 - 2 * xbit)
    lanes = ("y", "x", "z", "g", "c0", "c1", "c2", "c3")

    loads = [pltpu.make_async_copy(tok_hbm, tok, load_sem.at[4])]
    for kind in range(4):
        dst = own.at[kind] if kind < 3 else own_o
        loads.append(pltpu.make_async_copy(sources[kind], dst, load_sem.at[kind]))
    for copy in loads:
        copy.start()

    barrier = pltpu.get_barrier_semaphore()
    for slot in range(1, n):
        pl.semaphore_signal(barrier, inc=1, device_id={"dp": lax.rem(dp + slot, n)}, device_id_type=MESH)
    for step in range(steps):
        bit = lax.rem(seq // (1 << step), 2)
        mate = seq + (1 - 2 * bit) * (1 << step)
        pl.semaphore_signal(barrier, inc=1, device_id={"seq": mate}, device_id_type=MESH)
    pl.semaphore_wait(barrier, n - 1 + steps)

    def rows_of(kind, who, s):
        quarter = sources[kind].shape[0] // GROUP
        size = quarter // sub
        return pl.ds(pl.multiple_of(who * quarter + s * size, 16), size)

    def place(kind, slot, rows):
        if kind < 3:
            return wide.at[slot - 1, kind, rows, :]
        return wide_o.at[slot - 1, rows, :]

    pieces = [[(kind, slot, s) for s in range(sub) for slot in range(1, n)] for kind in range(4)]
    remote, sent = {}, []

    def push(src, dst, send, recv, target):
        copy = pltpu.make_async_remote_copy(
            src_ref=src, dst_ref=dst, send_sem=send, recv_sem=recv, device_id=target, device_id_type=MESH
        )
        copy.start()
        sent.append(copy)
        return copy

    for kind in range(4):
        for piece in pieces[kind]:
            _, slot, s = piece
            index = (0, kind, slot - 1, s)
            rows = rows_of(kind, rank, s)
            remote["y", piece] = push(
                sources[kind].at[rows, :], place(kind, slot, rows), sends.at[index], recvs.at[index],
                {"dp": lax.rem(dp - slot + n, n)},
            )

    def forward(name, piece, who, target):
        kind, slot, s = piece
        here = place(kind, slot, rows_of(kind, who, s))
        index = (lanes.index(name), kind, slot - 1, s)
        remote[name, piece] = push(here, here, sends.at[index], recvs.at[index], target)

    def relay(piece):
        remote["y", piece].wait_recv()
        forward("x", piece, rank, {"seq": x_mate})
        forward("z", piece, rank, {"seq": z_mate})
        forward("c0", piece, rank, {"seq": core_mate})

    def relay_again(piece):
        even = (piece[1] + piece[2]) % 2 == 1
        remote["x", piece].wait_recv()
        if even:
            forward("g", piece, x_rank, {"seq": z_mate})
        forward("c1", piece, x_rank, {"seq": core_mate})
        remote["z", piece].wait_recv()
        if not even:
            forward("g", piece, z_rank, {"seq": x_mate})
        forward("c2", piece, z_rank, {"seq": core_mate})

    def relay_last(piece):
        remote["g", piece].wait_recv()
        forward("c3", piece, g_rank, {"seq": core_mate})

    order = [piece for kind in range(4) for piece in pieces[kind]]
    half_of = len(pieces[0]) // 2 or 1
    cuts = [0]
    for kind in range(4):
        base = kind * len(pieces[0])
        cuts += [base + half_of, base + len(pieces[0])]
    acts = (relay, relay_again, relay_last)
    done = [0, 0, 0]

    def pump(*goals):
        goals = [cuts[goal] for goal in goals]
        while any(at < goal for at, goal in zip(done, goals)):
            todo = [i for i in range(3) if done[i] < goals[i] and (i == 0 or done[i] < done[i - 1])]
            pick = min(todo, key=lambda i: done[i] + 2 * half_of * i)
            acts[pick](order[done[pick]])
            done[pick] += 1

    def ready(kind):
        for piece in pieces[kind]:
            for name in ("c0", "c1", "c2", "c3"):
                remote[name, piece].wait_recv()

    chunk = min(256, cols)

    def project(kind, slot):
        source = own.at[kind] if slot == 0 else wide.at[slot - 1, kind]

        @pl.loop(0, cols // chunk)
        def _(i):
            at = pl.ds(pl.multiple_of(i * chunk, 128), chunk)
            kvq[kind, slot, :, at] = jnp.dot(tok[...], source[:, at], preferred_element_type=F32).astype(BF16)

    def states(slot, ref, base):
        @pl.loop(0, heads)
        def _(h):
            at = pl.ds(pl.multiple_of(h * DH, DH), DH)
            ref[pl.ds(pl.multiple_of(base + h * DH, DH), DH), :] = lax.dot_general(
                kvq[0, slot, :, at], kvq[1, slot, :, at], (((0,), (0,)), ((), ())), preferred_element_type=F32
            )

    half = length // 2

    def inner(slot):
        @pl.loop(0, heads)
        def _(h):
            at = pl.ds(pl.multiple_of(h * DH, DH), DH)
            for begin in (0, half):
                end = begin + half
                scores = lax.dot_general(
                    kvq[2, slot, begin:end, at], kvq[0, slot, :end, at], (((1,), (1,)), ((), ())),
                    preferred_element_type=F32,
                )
                row = begin + lax.broadcasted_iota(jnp.int32, (half, end), 0)
                col = lax.broadcasted_iota(jnp.int32, (half, end), 1)
                scores = jnp.where(col <= row, scores, 0.0).astype(BF16)
                within[slot, begin:end, at] = jnp.dot(
                    scores, kvq[1, slot, :end, at], preferred_element_type=F32
                )

    def finish(slot, prior, base):
        owner = lax.rem(dp + slot, n)

        @pl.loop(0, heads)
        def _(h):
            at = pl.ds(pl.multiple_of(h * DH, DH), DH)
            carried = jnp.dot(
                kvq[2, slot, :, at], prior[pl.ds(pl.multiple_of(base + h * DH, DH), DH), :],
                preferred_element_type=F32,
            )
            mixed = within[slot, :, at] + carried
            scale = lax.rsqrt(jnp.sum(mixed * mixed, axis=-1, keepdims=True) * (1.0 / DH) + 1e-05)
            normed[slot, :, at] = (mixed * scale * gain_ref[pl.ds(owner * heads + h, 1), :]).astype(BF16)

    def join(slot):
        source = own_o if slot == 0 else wide_o.at[slot - 1]

        @pl.loop(0, width // 256)
        def _(i):
            at = pl.ds(pl.multiple_of(i * 256, 128), 256)
            part = jnp.dot(normed[slot], source[:, at], preferred_element_type=F32)
            if slot > 0:
                part = acc[:, at] + part
            if slot == n - 1:
                out_ref[:, at] = part.astype(BF16)
            else:
                acc[:, at] = part

    scan_a = Scan(seq, steps, state_a, total_a, before_a, send_a, recv_a, prior_a, fin_a, as_send, as_recv)
    scan_b = Scan(seq, steps, state_b, total_b, before_b, send_b, recv_b, prior_b, fin_b, bs_send, bs_recv)

    others = range(1, n)
    loads[0].wait()
    loads[1].wait()
    project(0, 0)
    pump(1, 0, 0)
    loads[2].wait()
    project(1, 0)
    pump(2, 0, 0)
    states(0, state_a, 0)
    scan_a.begin()
    pump(3, 0, 0)
    loads[3].wait()
    project(2, 0)
    pump(4, 1, 0)
    scan_a.advance()
    inner(0)
    pump(5, 3, 1)
    scan_a.advance()
    pump(6, 4, 2)
    ready(0)
    for slot in others:
        project(0, slot)
    pump(7, 5, 3)
    scan_a.advance()
    pump(8, 6, 4)
    ready(1)
    for slot in others:
        project(1, slot)
        states(slot, state_b, (slot - 1) * cols)
    scan_b.begin()
    scan_a.advance()
    pump(8, 7, 5)
    scan_b.advance()
    scan_a.drain()
    finish(0, prior_a, 0)
    scan_b.advance()
    pump(8, 8, 6)
    loads[4].wait()
    join(0)
    scan_b.advance()
    ready(2)
    for slot in others:
        project(2, slot)
    pump(8, 8, 7)
    scan_b.advance()
    for slot in others:
        inner(slot)
    pump(8, 8, 8)
    scan_b.drain()
    for slot in others:
        finish(slot, prior_b, (slot - 1) * cols)
    ready(3)
    for slot in others:
        join(slot)
    for copy in sent:
        copy.wait_send()
    scan_a.close()
    scan_b.close()


def body(n, seqs, tokens, w_query, w_key, w_value, w_out, norm_gain):
    length, width = tokens.shape[1:]
    cols = w_query.shape[1]
    depth = w_out.shape[0]
    steps = seqs.bit_length() - 1
    sub = 2 if n <= 2 else 1
    any_spec = pl.BlockSpec(memory_space=pl.ANY)
    vmem = pl.BlockSpec(memory_space=pltpu.VMEM)
    scans = []
    for rows in (cols, (n - 1) * cols):
        part = rows // 2
        scans += [
            pltpu.VMEM((rows, DH), F32),
            pltpu.VMEM((part, DH), F32),
            pltpu.VMEM((part, DH), F32),
            pltpu.VMEM((steps, part, DH), BF16),
            pltpu.VMEM((steps, part, DH), BF16),
            pltpu.VMEM((rows, DH), BF16),
            pltpu.VMEM((part, DH), BF16),
        ]
    out = pl.pallas_call(
        functools.partial(kernel, n, steps, sub),
        out_shape=jax.ShapeDtypeStruct((length, width), BF16),
        in_specs=[any_spec] * 5 + [vmem],
        out_specs=vmem,
        scratch_shapes=[
            pltpu.VMEM((length, width), BF16),
            pltpu.VMEM((3, width, cols), BF16),
            pltpu.VMEM((depth, width), BF16),
            pltpu.VMEM((n - 1, 3, width, cols), BF16),
            pltpu.VMEM((n - 1, depth, width), BF16),
            pltpu.VMEM((3, n, length, cols), BF16),
            pltpu.VMEM((n, length, cols), F32),
            pltpu.VMEM((n, length, cols), BF16),
            pltpu.VMEM((length, width), F32),
        ]
        + scans
        + [pltpu.SemaphoreType.DMA((5,))]
        + [pltpu.SemaphoreType.DMA((8, 4, n - 1, sub))] * 2
        + [pltpu.SemaphoreType.DMA((steps + 1,))] * 4,
        compiler_params=pltpu.CompilerParams(
            collective_id=0, has_side_effects=True, vmem_limit_bytes=67043328
        ),
    )(tokens[0], w_query, w_key, w_value, w_out, norm_gain.reshape(-1, DH))
    return out[None]


def solution(mesh):
    in_specs = (
        P("dp", "seq", None),
        P(None, "dp"),
        P(None, "dp"),
        P(None, "dp"),
        P("dp", None),
        P(),
    )
    out_specs = P("dp", "seq", None)
    fn = functools.partial(body, mesh.shape["dp"], mesh.shape["seq"])
    return jax.shard_map(fn, mesh=mesh, in_specs=in_specs, out_specs=out_specs, check_vma=False)
```

```python
import functools

import jax
import jax.numpy as jnp
from jax import lax
from jax.experimental import pallas as pl
from jax.experimental.pallas import tpu as pltpu
from jax.sharding import PartitionSpec as P

H = 8
DH = 128
GROUP = 8
DIRECT = ((3, 1),)
MESH = pl.DeviceIdType.MESH
F32 = jnp.float32
BF16 = jnp.bfloat16


class Scan:
    def __init__(self, seq, steps, state, total, before, send, recv, prior, fin, send_sem, recv_sem):
        self.seq, self.steps = seq, steps
        self.state, self.total, self.before = state, total, before
        self.send, self.recv, self.prior, self.fin = send, recv, prior, fin
        self.send_sem, self.recv_sem = send_sem, recv_sem
        self.half = state.shape[0] // 2
        self.core = lax.rem(seq, 2)
        self.mine = pl.ds(pl.multiple_of(self.core * self.half, 16), self.half)
        self.other = pl.ds(pl.multiple_of((1 - self.core) * self.half, 16), self.half)
        self.at = 0
        self.copies = []

    def bit(self, step):
        return lax.rem(self.seq // (1 << step), 2)

    def partner(self, step):
        return self.seq + (1 - 2 * self.bit(step)) * (1 << step)

    def push(self, src, dst, index, step):
        copy = pltpu.make_async_remote_copy(
            src_ref=src,
            dst_ref=dst,
            send_sem=self.send_sem.at[index],
            recv_sem=self.recv_sem.at[index],
            device_id={"seq": self.partner(step)},
            device_id_type=MESH,
        )
        copy.start()
        self.copies.append(copy)

    def begin(self):
        self.send[0] = self.state[self.other, :].astype(BF16)
        self.push(self.send.at[0], self.recv.at[0], 0, 0)

    def advance(self):
        step = self.at
        if step > self.steps:
            return
        self.at += 1
        self.copies[step].wait_recv()
        if step == self.steps:
            return
        came = self.recv[step].astype(F32)
        if step == 0:
            self.total[...] = self.state[self.mine, :] + came
            self.before[...] = jnp.zeros(self.before.shape, F32)
        else:
            self.before[...] += jnp.where(self.bit(step) == 1, came, 0.0)
            if step < self.steps - 1:
                self.total[...] += came
        if step < self.steps - 1:
            self.send[step + 1] = self.total[...].astype(BF16)
            self.push(self.send.at[step + 1], self.recv.at[step + 1], step + 1, step + 1)
        else:
            before = self.before[...]
            first = self.recv[0].astype(F32)
            extra = jnp.where(self.core == 0, self.state[self.mine, :], 0.0)
            self.fin[...] = (before + extra).astype(BF16)
            self.push(self.fin, self.prior.at[self.mine, :], self.steps, 0)
            self.prior[self.mine, :] = (before + jnp.where(self.core == 1, first, 0.0)).astype(BF16)

    def drain(self):
        while self.at <= self.steps:
            self.advance()

    def close(self):
        for copy in self.copies:
            copy.wait_send()


def kernel(
    n, steps, sub,
    tok_hbm, wq_hbm, wk_hbm, wv_hbm, wo_hbm, gain_ref, out_ref,
    tok, own, own_o, wide, wide_o, kvq, within, normed, acc,
    state_a, total_a, before_a, send_a, recv_a, prior_a, fin_a,
    state_b, total_b, before_b, send_b, recv_b, prior_b, fin_b,
    load_sem, sends, recvs,
    as_send, as_recv, bs_send, bs_recv,
):
    dp, seq = lax.axis_index("dp"), lax.axis_index("seq")
    length, width = tok.shape
    cols = own.shape[2]
    heads = cols // DH
    sources = [wk_hbm, wv_hbm, wq_hbm, wo_hbm]
    rank = lax.rem(seq, GROUP)
    core = lax.rem(seq, 2)
    xbit = lax.rem(seq // 2, 2)
    core_mate = seq + 1 - 2 * core
    x_mate = seq + 2 * (1 - 2 * xbit)
    zbit = lax.rem(seq // 4, 2)
    z_mate = seq + 4 * (1 - 2 * zbit)
    x_rank = rank + 2 * (1 - 2 * xbit)
    z_rank = rank + 4 * (1 - 2 * zbit)
    g_rank = z_rank + 2 * (1 - 2 * xbit)
    lanes = ("y", "x", "z", "g", "c0", "c1", "c2", "c3")

    loads = [pltpu.make_async_copy(tok_hbm, tok, load_sem.at[4])]
    for kind in range(4):
        dst = own.at[kind] if kind < 3 else own_o
        loads.append(pltpu.make_async_copy(sources[kind], dst, load_sem.at[kind]))
    for copy in loads:
        copy.start()

    barrier = pltpu.get_barrier_semaphore()
    for slot in range(1, n):
        pl.semaphore_signal(barrier, inc=1, device_id={"dp": lax.rem(dp + slot, n)}, device_id_type=MESH)
    for step in range(steps):
        bit = lax.rem(seq // (1 << step), 2)
        mate = seq + (1 - 2 * bit) * (1 << step)
        pl.semaphore_signal(barrier, inc=1, device_id={"seq": mate}, device_id_type=MESH)
    pl.semaphore_wait(barrier, n - 1 + steps)

    def direct(kind, s):
        return (kind, s) in DIRECT

    def rows_of(kind, who, s):
        region = sources[kind].shape[0] // sub
        size = region // (2 if direct(kind, s) else GROUP)
        return pl.ds(pl.multiple_of(s * region + who * size, 16), size)

    def place(kind, slot, rows):
        if kind < 3:
            return wide.at[slot - 1, kind, rows, :]
        return wide_o.at[slot - 1, rows, :]

    pieces = [[(kind, slot, s) for s in range(sub) for slot in range(1, n)] for kind in range(4)]
    remote, sent = {}, []

    def push(src, dst, send, recv, target):
        copy = pltpu.make_async_remote_copy(
            src_ref=src, dst_ref=dst, send_sem=send, recv_sem=recv, device_id=target, device_id_type=MESH
        )
        copy.start()
        sent.append(copy)
        return copy

    for kind in range(4):
        for piece in pieces[kind]:
            _, slot, s = piece
            index = (0, kind, slot - 1, s)
            rows = rows_of(kind, core if direct(kind, s) else rank, s)
            remote["y", piece] = push(
                sources[kind].at[rows, :], place(kind, slot, rows), sends.at[index], recvs.at[index],
                {"dp": lax.rem(dp - slot + n, n)},
            )

    def forward(name, piece, who, target):
        kind, slot, s = piece
        here = place(kind, slot, rows_of(kind, who, s))
        index = (lanes.index(name), kind, slot - 1, s)
        remote[name, piece] = push(here, here, sends.at[index], recvs.at[index], target)

    def relay(piece):
        remote["y", piece].wait_recv()
        if direct(piece[0], piece[2]):
            forward("c0", piece, core, {"seq": core_mate})
            return
        forward("x", piece, rank, {"seq": x_mate})
        forward("z", piece, rank, {"seq": z_mate})
        forward("c0", piece, rank, {"seq": core_mate})

    def relay_again(piece):
        if direct(piece[0], piece[2]):
            return
        even = (piece[1] + piece[2]) % 2 == 1
        remote["x", piece].wait_recv()
        if even:
            forward("g", piece, x_rank, {"seq": z_mate})
        forward("c1", piece, x_rank, {"seq": core_mate})
        remote["z", piece].wait_recv()
        if not even:
            forward("g", piece, z_rank, {"seq": x_mate})
        forward("c2", piece, z_rank, {"seq": core_mate})

    def relay_last(piece):
        if direct(piece[0], piece[2]):
            return
        remote["g", piece].wait_recv()
        forward("c3", piece, g_rank, {"seq": core_mate})

    order = [piece for kind in range(4) for piece in pieces[kind]]
    half_of = len(pieces[0]) // 2 or 1
    cuts = [0]
    for kind in range(4):
        base = kind * len(pieces[0])
        cuts += [base + half_of, base + len(pieces[0])]
    acts = (relay, relay_again, relay_last)
    done = [0, 0, 0]

    def pump(*goals):
        goals = [cuts[goal] for goal in goals]
        while any(at < goal for at, goal in zip(done, goals)):
            todo = [i for i in range(3) if done[i] < goals[i] and (i == 0 or done[i] < done[i - 1])]
            pick = min(todo, key=lambda i: done[i] + 2 * half_of * i)
            acts[pick](order[done[pick]])
            done[pick] += 1

    def ready(kind):
        for piece in pieces[kind]:
            for name in ("c0",) if direct(kind, piece[2]) else ("c0", "c1", "c2", "c3"):
                remote[name, piece].wait_recv()

    chunk = min(256, cols)

    def project(kind, slot):
        source = own.at[kind] if slot == 0 else wide.at[slot - 1, kind]

        @pl.loop(0, cols // chunk)
        def _(i):
            at = pl.ds(pl.multiple_of(i * chunk, 128), chunk)
            kvq[kind, slot, :, at] = jnp.dot(tok[...], source[:, at], preferred_element_type=F32).astype(BF16)

    def states(slot, ref, base):
        @pl.loop(0, heads)
        def _(h):
            at = pl.ds(pl.multiple_of(h * DH, DH), DH)
            ref[pl.ds(pl.multiple_of(base + h * DH, DH), DH), :] = lax.dot_general(
                kvq[0, slot, :, at], kvq[1, slot, :, at], (((0,), (0,)), ((), ())), preferred_element_type=F32
            )

    half = length // 2

    def inner(slot):
        @pl.loop(0, heads)
        def _(h):
            at = pl.ds(pl.multiple_of(h * DH, DH), DH)
            for begin in (0, half):
                end = begin + half
                scores = lax.dot_general(
                    kvq[2, slot, begin:end, at], kvq[0, slot, :end, at], (((1,), (1,)), ((), ())),
                    preferred_element_type=F32,
                )
                row = begin + lax.broadcasted_iota(jnp.int32, (half, end), 0)
                col = lax.broadcasted_iota(jnp.int32, (half, end), 1)
                scores = jnp.where(col <= row, scores, 0.0).astype(BF16)
                within[slot, begin:end, at] = jnp.dot(
                    scores, kvq[1, slot, :end, at], preferred_element_type=F32
                )

    def finish(slot, prior, base):
        owner = lax.rem(dp + slot, n)

        @pl.loop(0, heads)
        def _(h):
            at = pl.ds(pl.multiple_of(h * DH, DH), DH)
            carried = jnp.dot(
                kvq[2, slot, :, at], prior[pl.ds(pl.multiple_of(base + h * DH, DH), DH), :],
                preferred_element_type=F32,
            )
            mixed = within[slot, :, at] + carried
            scale = lax.rsqrt(jnp.sum(mixed * mixed, axis=-1, keepdims=True) * (1.0 / DH) + 1e-05)
            normed[slot, :, at] = (mixed * scale * gain_ref[pl.ds(owner * heads + h, 1), :]).astype(BF16)

    def join(slot):
        source = own_o if slot == 0 else wide_o.at[slot - 1]

        @pl.loop(0, width // 256)
        def _(i):
            at = pl.ds(pl.multiple_of(i * 256, 128), 256)
            part = jnp.dot(normed[slot], source[:, at], preferred_element_type=F32)
            if slot > 0:
                part = acc[:, at] + part
            if slot == n - 1:
                out_ref[:, at] = part.astype(BF16)
            else:
                acc[:, at] = part

    scan_a = Scan(seq, steps, state_a, total_a, before_a, send_a, recv_a, prior_a, fin_a, as_send, as_recv)
    scan_b = Scan(seq, steps, state_b, total_b, before_b, send_b, recv_b, prior_b, fin_b, bs_send, bs_recv)

    others = range(1, n)
    loads[0].wait()
    loads[1].wait()
    project(0, 0)
    pump(1, 0, 0)
    loads[2].wait()
    project(1, 0)
    pump(2, 0, 0)
    states(0, state_a, 0)
    scan_a.begin()
    pump(3, 0, 0)
    loads[3].wait()
    project(2, 0)
    pump(4, 1, 0)
    scan_a.advance()
    inner(0)
    pump(5, 3, 1)
    scan_a.advance()
    pump(6, 4, 2)
    ready(0)
    for slot in others:
        project(0, slot)
    pump(7, 5, 3)
    scan_a.advance()
    pump(8, 6, 4)
    ready(1)
    for slot in others:
        project(1, slot)
        states(slot, state_b, (slot - 1) * cols)
    scan_b.begin()
    scan_a.advance()
    pump(8, 7, 5)
    scan_b.advance()
    scan_a.drain()
    finish(0, prior_a, 0)
    scan_b.advance()
    pump(8, 8, 6)
    loads[4].wait()
    join(0)
    scan_b.advance()
    ready(2)
    for slot in others:
        project(2, slot)
    pump(8, 8, 7)
    scan_b.advance()
    for slot in others:
        inner(slot)
    pump(8, 8, 8)
    scan_b.drain()
    for slot in others:
        finish(slot, prior_b, (slot - 1) * cols)
    ready(3)
    for slot in others:
        join(slot)
    for copy in sent:
        copy.wait_send()
    scan_a.close()
    scan_b.close()


def body(n, seqs, tokens, w_query, w_key, w_value, w_out, norm_gain):
    length, width = tokens.shape[1:]
    cols = w_query.shape[1]
    depth = w_out.shape[0]
    steps = seqs.bit_length() - 1
    sub = 2 if n <= 2 else 1
    any_spec = pl.BlockSpec(memory_space=pl.ANY)
    vmem = pl.BlockSpec(memory_space=pltpu.VMEM)
    scans = []
    for rows in (cols, (n - 1) * cols):
        part = rows // 2
        scans += [
            pltpu.VMEM((rows, DH), F32),
            pltpu.VMEM((part, DH), F32),
            pltpu.VMEM((part, DH), F32),
            pltpu.VMEM((steps, part, DH), BF16),
            pltpu.VMEM((steps, part, DH), BF16),
            pltpu.VMEM((rows, DH), BF16),
            pltpu.VMEM((part, DH), BF16),
        ]
    out = pl.pallas_call(
        functools.partial(kernel, n, steps, sub),
        out_shape=jax.ShapeDtypeStruct((length, width), BF16),
        in_specs=[any_spec] * 5 + [vmem],
        out_specs=vmem,
        scratch_shapes=[
            pltpu.VMEM((length, width), BF16),
            pltpu.VMEM((3, width, cols), BF16),
            pltpu.VMEM((depth, width), BF16),
            pltpu.VMEM((n - 1, 3, width, cols), BF16),
            pltpu.VMEM((n - 1, depth, width), BF16),
            pltpu.VMEM((3, n, length, cols), BF16),
            pltpu.VMEM((n, length, cols), F32),
            pltpu.VMEM((n, length, cols), BF16),
            pltpu.VMEM((length, width), F32),
        ]
        + scans
        + [pltpu.SemaphoreType.DMA((5,))]
        + [pltpu.SemaphoreType.DMA((8, 4, n - 1, sub))] * 2
        + [pltpu.SemaphoreType.DMA((steps + 1,))] * 4,
        compiler_params=pltpu.CompilerParams(
            collective_id=0, has_side_effects=True, vmem_limit_bytes=67043328
        ),
    )(tokens[0], w_query, w_key, w_value, w_out, norm_gain.reshape(-1, DH))
    return out[None]


def solution(mesh):
    in_specs = (
        P("dp", "seq", None),
        P(None, "dp"),
        P(None, "dp"),
        P(None, "dp"),
        P("dp", None),
        P(),
    )
    out_specs = P("dp", "seq", None)
    fn = functools.partial(body, mesh.shape["dp"], mesh.shape["seq"])
    return jax.shard_map(fn, mesh=mesh, in_specs=in_specs, out_specs=out_specs, check_vma=False)
```
